128 devices in a mesh: req: 4 (over z_lo, core), seq: 32 (over y, x, z_hi).
Axes of the slice: x: 4, y: 4, z: 4 (z_hi: 2, z_lo: 2; z = z_hi * 2 + z_lo), core: 2. Of those that a mesh axis runs over, the one named last changes fastest.
Arguments:
- prefill_query: bfloat16 [16384, 1536], P(('req', 'seq')), may hold values from -512 to 512
- prefill_key: bfloat16 [16384, 512], P(('req', 'seq')), may hold values from -512 to 512
- prefill_value: bfloat16 [16384, 512], P(('req', 'seq')), may hold values from -6 to 6
- prefill_resid: bfloat16 [16384, 1536], P(('req', 'seq')), may hold values from -6 to 6
- dec_query: bfloat16 [16, 1536], P('req'), may hold values from -512 to 512
- dec_key_new: bfloat16 [16, 512], P('req'), may hold values from -16 to 16
- dec_value_new: bfloat16 [16, 512], P('req'), may hold values from -6 to 6
- dec_resid: bfloat16 [16, 1536], P('req'), may hold values from -6 to 6
- cache_lengths: int32 [16], P('req'), may hold values from 16 to 32768, as said below
- key_cache: bfloat16 [16, 32768, 512], P('req', 'seq'), may hold values from -512 to 512
- value_cache: bfloat16 [16, 32768, 512], P('req', 'seq'), may hold values from -6 to 6
- attn_out_weight: bfloat16 [1536, 1536], replicated, may hold values from -0.15625 to 0.15625
- ffn_gain: float32 [1536], replicated, may hold values from 0.1 to 1.9
- expert_gate: bfloat16 [32, 1536, 512], P('seq', 'req'), may hold values from -0.15625 to 0.15625
- expert_up: bfloat16 [32, 1536, 512], P('seq', 'req'), may hold values from -0.15625 to 0.15625
- expert_down: bfloat16 [32, 512, 1536], P('seq', None, 'req'), may hold values from -0.25 to 0.25
- routes: int32 [16384, 8], P(('req', 'seq')), may hold values from 0 to 31, all different within a row; in each aligned block of 128 rows (0 to 127, 128 to 255, ...) at most 40 rows name the same one
- route_weights: float32 [16384, 8], P(('req', 'seq')), may hold values from 0.05 to 0.5
Outputs:
- prefill_out: bfloat16 [16384, 1536], P(('req', 'seq'))
- dec_out: bfloat16 [16, 1536], P('req')
The draws below stay inside these ranges and needn't reach their ends.
Inputs may be any that keep to these rules, and one draw needn't show every extreme that they name: `routes`: in each aligned block of 128 rows (the rows of one device) no expert is named by more than 40 rows. `cache_lengths`: some request uses all 32768 positions.
All inputs are finite; a program needn't handle non-finite values.
Results may differ from the reference program's by a relative error of at most 0.012.
Values may be sent and summed in bfloat16 or wider, within the bound.
No kernel may reach another device: no remote copies, remote signals or barrier semaphores. Data moves between devices by JAX's collectives and lax.ppermute only.
A program may use at most 128 MiB of HBM per device.

```python
import math
import jax
import jax.numpy as jnp
import numpy as np
from jax import lax

D = 1536
HEADS = 24
KVH = 8
HD = 64
FFE = 512
EXPERTS = 32
TOP = 8
TOK_DEV = 128
CBLK = 1024
SPAN = 4096
PTOK = 16384
DREQ = 16
MAXLEN = 32768
CAP = 40


def prefill_pair(key):
    key_query = jax.random.fold_in(key, 11)
    key_keys = jax.random.fold_in(key, 12)
    query_rows = jax.random.truncated_normal(key_query, -6.0, 6.0, (PTOK, HEADS * HD), jnp.float32)
    key_rows = jax.random.truncated_normal(key_keys, -6.0, 6.0, (PTOK, KVH * HD), jnp.float32)
    return (query_rows, key_rows)


def draw_prefill_query(key, part):
    return prefill_pair(key)[0].astype(jnp.bfloat16)


def draw_prefill_key(key, part):
    return prefill_pair(key)[1].astype(jnp.bfloat16)


def decode_pair(key):
    cache_rows = jax.random.truncated_normal(jax.random.fold_in(key, 21), -6.0, 6.0, (DREQ, MAXLEN, KVH * HD), jnp.float32)
    query_rows = jax.random.truncated_normal(jax.random.fold_in(key, 22), -6.0, 6.0, (DREQ, HEADS * HD), jnp.float32)
    request_ids = jnp.arange(DREQ, dtype=jnp.int32)
    lengths = draw_cache_lengths(key, 0)
    anywhere = jax.random.randint(jax.random.fold_in(key, 25), (DREQ,), 0, lengths)
    far_block = MAXLEN // 2 + jax.random.randint(jax.random.fold_in(key, 26), (DREQ,), 0, CBLK)
    place = jnp.where(lengths > MAXLEN // 2, far_block, anywhere)
    group_mean = jnp.mean(query_rows.reshape(DREQ, KVH, HEADS // KVH, HD), axis=2).reshape(DREQ, KVH * HD)
    cache_rows = cache_rows.at[request_ids, place].set(6.0 * group_mean)
    return (query_rows, cache_rows)


def draw_dec_query(key, part):
    return decode_pair(key)[0].astype(jnp.bfloat16)


def draw_key_cache(key, part):
    return decode_pair(key)[1].astype(jnp.bfloat16)


def draw_cache_lengths(key, part):
    doubling = jax.random.randint(jax.random.fold_in(key, 31), (DREQ,), 0, 12)
    upper = jnp.minimum(jnp.left_shift(jnp.int32(16), doubling), MAXLEN)
    lengths = jax.random.randint(jax.random.fold_in(key, 32), (DREQ,), 16, upper + 1)
    full_index = jax.random.randint(jax.random.fold_in(key, 33), (), 0, DREQ)
    return lengths.at[full_index].set(MAXLEN).astype(jnp.int32)


def level_of(own_key, dims, split, least, top_value):
    factor_of = 1.0
    for axis_at, shards_of in split:
        steps = jax.random.uniform(jax.random.fold_in(jax.random.fold_in(own_key, 6), axis_at), (shards_of,), jnp.float32, least / len(split), top_value / len(split))
        factor_of = factor_of * jnp.repeat(jnp.exp(steps), dims[axis_at] // shards_of).reshape((-1,) + (1,) * (len(dims) - 1 - axis_at))
    return factor_of


def assign_block(key, own, number, rows, number_of, top, bound, lean):
    ranking = jax.random.permutation(key, number_of)
    heavy_load, common = shares(number_of, rows * top, bound, lean, True), shares(number_of, rows * top, bound, lean, False)
    places = jnp.arange(number_of)

    def named(sizes, rotation):
        used = int((sizes > 0).sum())
        fixed = max(1, used // 4)
        passed = fixed + (places - fixed + rotation * (used - fixed)) % max(1, number_of - fixed)
        return jnp.zeros((number_of,), jnp.int32).at[ranking[jnp.where(places < fixed, places, passed)]].set(jnp.asarray(sizes, jnp.int32))

    sizes = jnp.where(number % 4 == 0, named(heavy_load, number // 4), named(common, number - number // 4 - 1))
    mixed = jax.random.permutation(jax.random.fold_in(own, 3), number_of)
    donor, receiver = mixed[0:number_of // 2 * 2:2], mixed[1:number_of // 2 * 2:2]
    room = jnp.minimum(sizes[donor] - 1, bound - sizes[receiver]) // 2
    room = jnp.where((donor == ranking[0]) | (receiver == ranking[0]) | (sizes[receiver] == 0), 0, jnp.maximum(room, 0))
    passed = jax.random.randint(jax.random.fold_in(own, 4), (number_of // 2,), 0, 1 << 20) % (room + 1)
    sizes = sizes.at[donor].add(-passed).at[receiver].add(passed)
    labels = jnp.searchsorted(jnp.cumsum(sizes), jnp.arange(rows * top), side="right").astype(jnp.int32)
    grid = labels.reshape(top, rows).T
    grid = grid[jax.random.permutation(jax.random.fold_in(own, 1), rows)]
    rotation = jax.random.randint(jax.random.fold_in(own, 2), (rows, 1), 0, top)
    return jnp.take_along_axis(grid, (jnp.arange(top)[None, :] + rotation) % top, axis=1)


def shares(amount, total, bound, lean, full):
    loads = [(1 << 20) // math.isqrt(standing ** lean) + 1 for standing in range(1, amount + 1)]
    largest = bound if full else min(bound, max(-(-total // amount), total * loads[0] // sum(loads)))
    least = 1 if total - largest >= amount - 1 else 0
    given, surplus = [largest] + [least] * (amount - 1), total - largest - least * (amount - 1)
    while surplus > 0:
        free = [i for i in range(1, amount) if given[i] < largest] or [i for i in range(1, amount) if given[i] < bound]
        pool, left = sum([loads[i] for i in free]), surplus
        for i in free:
            extra = min(bound - given[i], max(1, left * loads[i] // pool), surplus)
            given[i] = given[i] + extra
            surplus = surplus - extra
    return np.array(given)


def gaussian(stream_key, shape, spread, most, cuts=(), kind=jnp.bfloat16):
    drawn = spread * jax.random.normal(stream_key, shape, jnp.float32)
    if cuts:
        drawn = drawn * level_of(stream_key, shape, cuts, -0.22, 0.18)
    return jnp.clip(drawn, -most, most).astype(kind)


def setup_inputs(seed: int = 0) -> dict:
    arg_keys = jax.random.split(jax.random.key(seed), 19)
    prefill_query = draw_prefill_query(jax.random.fold_in(arg_keys[18], 71), 0)
    prefill_key = draw_prefill_key(jax.random.fold_in(arg_keys[18], 71), 0)
    prefill_value = gaussian(arg_keys[2], (PTOK, KVH * HD), 1.0, 6.0, ((0, 128),))
    prefill_resid = gaussian(arg_keys[3], (PTOK, D), 1.0, 6.0, ((0, 128),))
    dec_query = draw_dec_query(jax.random.fold_in(arg_keys[18], 71), 0)
    dec_key_new = gaussian(arg_keys[5], (DREQ, KVH * HD), 4.0, 16.0, ((0, 4),))
    dec_value_new = gaussian(arg_keys[6], (DREQ, KVH * HD), 1.0, 6.0, ((0, 4),))
    dec_resid = gaussian(arg_keys[7], (DREQ, D), 1.0, 6.0, ((0, 4),))
    cache_lengths = draw_cache_lengths(jax.random.fold_in(arg_keys[18], 71), 0)
    key_cache = draw_key_cache(jax.random.fold_in(arg_keys[18], 71), 0)
    value_cache = gaussian(arg_keys[10], (DREQ, MAXLEN, KVH * HD), 1.0, 6.0, ((0, 4), (1, 32)))
    attn_out_weight = gaussian(arg_keys[11], (HEADS * HD, D), (HEADS * HD) ** -0.5, 0.15625)
    ffn_gain = jnp.clip(1.0 + 0.18 * jax.random.normal(arg_keys[12], (D,), jnp.float32), 0.1, 1.9)
    expert_gate = gaussian(arg_keys[13], (EXPERTS, D, FFE), D ** -0.5, 0.15625, ((0, 32), (1, 4)))
    expert_up = gaussian(arg_keys[14], (EXPERTS, D, FFE), D ** -0.5, 0.15625, ((0, 32), (1, 4)))
    expert_down = gaussian(arg_keys[15], (EXPERTS, FFE, D), FFE ** -0.5, 0.25, ((0, 32), (2, 4)))
    routes_keys = jax.random.split(jax.random.fold_in(arg_keys[16], 1), PTOK // TOK_DEV)
    routes_turns = jax.random.permutation(jax.random.fold_in(arg_keys[16], 3), PTOK // TOK_DEV)
    routes = jax.vmap(lambda own, number: assign_block(jax.random.fold_in(arg_keys[16], 2), own, number, TOK_DEV, EXPERTS, TOP, CAP, 1))(routes_keys, routes_turns).reshape((PTOK, TOP))
    route_weights = jnp.clip(jnp.exp(math.log(0.5) - 2.3025851 * jax.random.uniform(arg_keys[17], (PTOK, TOP), jnp.float32) ** level_of(arg_keys[17], (PTOK, TOP), ((0, 128),), -0.2, 0.2)), 0.05, 0.5)
    return dict(prefill_query=prefill_query, prefill_key=prefill_key, prefill_value=prefill_value, prefill_resid=prefill_resid, dec_query=dec_query, dec_key_new=dec_key_new, dec_value_new=dec_value_new, dec_resid=dec_resid, cache_lengths=cache_lengths, key_cache=key_cache, value_cache=value_cache, attn_out_weight=attn_out_weight, ffn_gain=ffn_gain, expert_gate=expert_gate, expert_up=expert_up, expert_down=expert_down, routes=routes, route_weights=route_weights)


NEGATIVE = -1e+30
EPSILON = 1e-05

def span_attention(pieces):
    query_rows, key_rows, value_rows = pieces
    group_size = HEADS // KVH
    score_scale = 1.0 / math.sqrt(HD)
    block_rows = math.gcd(SPAN, 512)
    query_heads = query_rows.reshape(SPAN, KVH, group_size, HD).astype(jnp.float32)
    key_heads = key_rows.reshape(SPAN, KVH, HD).astype(jnp.float32)
    value_heads = value_rows.reshape(SPAN, KVH, HD).astype(jnp.float32)
    outputs = []
    for number in range(SPAN // block_rows):
        key_reach = (number + 1) * block_rows
        query_block = query_heads[number * block_rows:key_reach]
        scores = jnp.einsum('qkgd,pkd->qkgp', query_block, key_heads[:key_reach]) * score_scale
        row_index = number * block_rows + jnp.arange(block_rows, dtype=jnp.int32)
        column_index = jnp.arange(key_reach, dtype=jnp.int32)
        visible = (column_index[None, :] <= row_index[:, None])[:, None, None, :]
        scores = jnp.where(visible, scores, NEGATIVE)
        row_top = lax.optimization_barrier(jnp.max(scores, axis=-1, keepdims=True))
        exponent = jnp.where(visible, jnp.exp(scores - row_top), 0.0)
        row_total = lax.optimization_barrier(jnp.sum(exponent, axis=-1))
        weights = lax.optimization_barrier(exponent.astype(jnp.bfloat16)).astype(jnp.float32)
        numerator = jnp.einsum('qkgp,pkd->qkgd', weights, value_heads[:key_reach])
        outputs.append((numerator / row_total[..., None]).reshape(block_rows, HEADS * HD))
    return jnp.concatenate(outputs, 0).astype(jnp.bfloat16)

def decode_request(pieces):
    query_row, key_fresh, value_fresh, length, key_rows, value_rows = pieces
    group_size = HEADS // KVH
    score_scale = 1.0 / math.sqrt(HD)
    query_heads = query_row.reshape(KVH, group_size, HD).astype(jnp.float32)
    key_heads = key_rows.reshape(MAXLEN, KVH, HD).astype(jnp.float32)
    value_heads = value_rows.reshape(MAXLEN, KVH, HD).astype(jnp.float32)
    scores = jnp.einsum('kgd,pkd->kgp', query_heads, key_heads) * score_scale
    visible = (jnp.arange(MAXLEN, dtype=jnp.int32) < length)[None, None, :]
    scores = jnp.where(visible, scores, NEGATIVE)
    fresh_score = jnp.einsum('kgd,kd->kg', query_heads, key_fresh.reshape(KVH, HD).astype(jnp.float32)) * score_scale
    row_top = jnp.maximum(lax.optimization_barrier(jnp.max(scores, axis=-1)), fresh_score)
    exponent = jnp.where(visible, jnp.exp(scores - row_top[..., None]), 0.0)
    fresh_exp = jnp.exp(fresh_score - row_top)
    denominator = lax.optimization_barrier(jnp.sum(exponent, axis=-1)) + fresh_exp
    weights = lax.optimization_barrier(exponent.astype(jnp.bfloat16)).astype(jnp.float32)
    fresh_weight = lax.optimization_barrier(fresh_exp.astype(jnp.bfloat16)).astype(jnp.float32)
    numerator = jnp.einsum('kgp,pkd->kgd', weights, value_heads)
    numerator = numerator + fresh_weight[..., None] * value_fresh.reshape(KVH, 1, HD).astype(jnp.float32)
    return (numerator / denominator[..., None]).reshape(HEADS * HD).astype(jnp.bfloat16)

def rms_scale(hidden, gain):
    values_float = hidden.astype(jnp.float32)
    mean_square = lax.optimization_barrier(jnp.mean(values_float * values_float, axis=-1, keepdims=True))
    return (values_float * lax.rsqrt(mean_square + EPSILON) * gain).astype(jnp.bfloat16)

def expert_mixture(normed, routes, route_weights, expert_gate, expert_up, expert_down):
    blocks = PTOK // TOK_DEV
    flat_expert = routes.reshape(blocks, TOK_DEV * TOP)
    onehot = (flat_expert[..., None] == jnp.arange(EXPERTS, dtype=jnp.int32)).astype(jnp.int32)
    earlier = jnp.cumsum(onehot, axis=1) - onehot
    slot_index = lax.optimization_barrier(jnp.sum(earlier * onehot, axis=-1)).reshape(-1).astype(jnp.int32)
    token_index = (jnp.arange(PTOK * TOP, dtype=jnp.int32) // TOP).astype(jnp.int32)
    block_index = (token_index // TOK_DEV).astype(jnp.int32)
    expert_index = routes.reshape(-1).astype(jnp.int32)
    slot_table = jnp.zeros((EXPERTS, blocks, CAP), jnp.int32).at[expert_index, block_index, slot_index].set(token_index)
    scales = jnp.zeros((EXPERTS, blocks, CAP), jnp.float32).at[expert_index, block_index, slot_index].set(route_weights.reshape(-1))

    def one_expert(combined, pieces):
        rows_table, rows_scale, gate_matrix, up_matrix, down_matrix = pieces
        flat_rows = rows_table.reshape(-1)
        inputs = normed[flat_rows]
        gate_value = jnp.dot(inputs, gate_matrix, preferred_element_type=jnp.float32)
        up_value = jnp.dot(inputs, up_matrix, preferred_element_type=jnp.float32)
        hidden = (jax.nn.silu(gate_value) * up_value).astype(jnp.bfloat16)
        output = jnp.dot(hidden, down_matrix, preferred_element_type=jnp.float32).astype(jnp.bfloat16)
        combined = combined.at[flat_rows].add(rows_scale.reshape(-1)[:, None] * output.astype(jnp.float32))
        return (combined, None)
    combined, unused = lax.scan(one_expert, jnp.zeros((PTOK, D), jnp.float32), (slot_table, scales, expert_gate, expert_up, expert_down))
    return combined

def reference(prefill_query, prefill_key, prefill_value, prefill_resid, dec_query, dec_key_new, dec_value_new, dec_resid, cache_lengths, key_cache, value_cache, attn_out_weight, ffn_gain, expert_gate, expert_up, expert_down, routes, route_weights):
    spans = PTOK // SPAN
    attended = lax.map(span_attention, (prefill_query.reshape(spans, SPAN, HEADS * HD), prefill_key.reshape(spans, SPAN, KVH * HD), prefill_value.reshape(spans, SPAN, KVH * HD)))
    attended = attended.reshape(PTOK, HEADS * HD)
    middle = (prefill_resid.astype(jnp.float32) + jnp.dot(attended, attn_out_weight, preferred_element_type=jnp.float32)).astype(jnp.bfloat16)
    normed = rms_scale(middle, ffn_gain)
    mixture = expert_mixture(normed, routes, route_weights, expert_gate, expert_up, expert_down)
    prefill_out = (middle.astype(jnp.float32) + mixture).astype(jnp.bfloat16)
    decoded = lax.map(decode_request, (dec_query, dec_key_new, dec_value_new, cache_lengths, key_cache, value_cache))
    dec_out = (dec_resid.astype(jnp.float32) + jnp.dot(decoded, attn_out_weight, preferred_element_type=jnp.float32)).astype(jnp.bfloat16)
    return (prefill_out, dec_out)
```

```python
import jax
import jax.numpy as jnp
from jax import lax
from jax.experimental import pallas as pl
from jax.experimental.pallas import tpu as pltpu
from jax.sharding import PartitionSpec as P

D = 1536
HEADS = 24
KVH = 8
GROUP = HEADS // KVH
HD = 64
FFE = 512
EXPERTS = 32
CAP = 40
TOK = 128
SEQ = 32
PARTS = SEQ // KVH
STRIP = TOK // PARTS
HALF = STRIP // 2
QROWS = GROUP * HALF
PACK = TOK + QROWS
SLOTS = EXPERTS * CAP
CBLK = 1024
RLOC = 4

NEGATIVE = -1e30
EPSILON = 1e-05
SCALE = 0.125
F32 = jnp.float32
BF16 = jnp.bfloat16
MIB = 1 << 20


def swap_halves(x):
    return jnp.concatenate([x[..., HD:], x[..., :HD]], axis=-1)


def left_lanes(shape):
    return lax.broadcasted_iota(jnp.int32, shape, len(shape) - 1) < HD


def dot_nt(a, b):
    return lax.dot_general(a, b, (((1,), (1,)), ((), ())), preferred_element_type=F32)


def dot_nn(a, b):
    return lax.dot_general(a, b, (((1,), (0,)), ((), ())), preferred_element_type=F32)


def pack_kernel(q_ref, k_ref, v_ref, o_ref):
    left = left_lanes((TOK, 2 * HD))
    for pair in range(KVH // 2):
        lanes = slice(pair * 128, pair * 128 + 128)
        keys, values = k_ref[:, lanes], v_ref[:, lanes]
        even = jnp.where(left, keys, swap_halves(values))
        odd = jnp.where(left, swap_halves(keys), values)
        for part in range(PARTS):
            o_ref[2 * pair * PARTS + part, :TOK, :] = even
            o_ref[(2 * pair + 1) * PARTS + part, :TOK, :] = odd
    left = left_lanes((PARTS * HALF, 2 * HD))
    for pair in range(HEADS // 2):
        rows = q_ref[:, pair * 128 : pair * 128 + 128] * jnp.asarray(SCALE, BF16)
        rows = rows.reshape(PARTS, 2, HALF, 128)
        top = rows[:, 0].reshape(PARTS * HALF, 128)
        bottom = rows[:, 1].reshape(PARTS * HALF, 128)
        even = jnp.where(left, top, swap_halves(bottom))
        odd = jnp.where(left, swap_halves(top), bottom)
        for head, packed in ((2 * pair, even), (2 * pair + 1, odd)):
            kv, group = head // GROUP, head % GROUP
            for part in range(PARTS):
                o_ref[
                    kv * PARTS + part, TOK + group * HALF : TOK + (group + 1) * HALF, :
                ] = packed[part * HALF : (part + 1) * HALF]


def pack(query, key, value):
    return pl.pallas_call(
        pack_kernel,
        out_shape=jax.ShapeDtypeStruct((SEQ, PACK, 128), BF16),
        compiler_params=pltpu.CompilerParams(vmem_limit_bytes=32 * MIB),
        name="pack",
    )(query, key, value)


QS = 8
KS = 8
TILE = QS * 2 * QROWS
KBLK = KS * TOK


def attention_kernel(strip_ref, x_ref, o_ref, ones_ref, q_ref, m_ref, acc_ref):
    strip = strip_ref[0]
    for block in range(SEQ // KS):
        kv = x_ref[block * KS : (block + 1) * KS, :TOK, :].reshape(KBLK, 128)
        ones_ref[block] = jnp.where(left_lanes((KBLK, 128)), jnp.asarray(1.0, BF16), kv)
    half = QS * QROWS
    left = left_lanes((half, 128))
    row = lax.broadcasted_iota(jnp.int32, (TILE, KBLK), 0)
    lower = row >= half
    row = jnp.where(lower, row - half, row)
    source = row // QROWS
    inner = row % HALF
    position = source * TOK + strip * STRIP + inner + jnp.where(lower, HALF, 0)
    key_position = lax.broadcasted_iota(jnp.int32, (TILE, KBLK), 1)
    visible = key_position <= position

    def step(block, masked):
        kv = x_ref[pl.ds(block * KS, KS), :TOK, :].reshape(KBLK, 128)
        scores = dot_nt(q_ref[...], kv)
        if masked:
            scores = jnp.where(visible, scores, NEGATIVE)
        before = m_ref[...]
        top = jnp.maximum(before, jnp.max(scores, axis=1, keepdims=True))
        weights = jnp.exp(scores - top[:, :1]).astype(BF16)
        acc_ref[...] = acc_ref[...] * jnp.exp(before - top) + dot_nn(weights, ones_ref[block])
        m_ref[...] = top

    def tile(number, carry):
        packed = x_ref[pl.ds(number * QS, QS), TOK:, :].reshape(half, 128)
        zero = jnp.zeros_like(packed)
        q_ref[:half] = jnp.where(left, packed, zero)
        q_ref[half:] = jnp.where(left, swap_halves(packed), zero)
        m_ref[...] = jnp.full((TILE, 128), NEGATIVE, F32)
        acc_ref[...] = jnp.zeros((TILE, 128), F32)

        def block(index, inner_carry):
            step(index, False)
            return inner_carry

        lax.fori_loop(0, number, block, 0)
        step(number, True)
        total = acc_ref[...]
        result = total / swap_halves(total)
        merged = jnp.where(left, swap_halves(result[:half]), result[half:])
        o_ref[pl.ds(number * QS, QS)] = merged.astype(BF16).reshape(QS, QROWS, 128)
        return carry

    lax.fori_loop(0, SEQ // QS, tile, 0)


def attention(strip, received):
    return pl.pallas_call(
        attention_kernel,
        out_shape=jax.ShapeDtypeStruct((SEQ, QROWS, 128), BF16),
        in_specs=[
            pl.BlockSpec(memory_space=pltpu.SMEM),
            pl.BlockSpec(memory_space=pltpu.VMEM),
        ],
        scratch_shapes=[
            pltpu.VMEM((SEQ // KS, KBLK, 128), BF16),
            pltpu.VMEM((TILE, 128), BF16),
            pltpu.VMEM((TILE, 128), F32),
            pltpu.VMEM((TILE, 128), F32),
        ],
        compiler_params=pltpu.CompilerParams(vmem_limit_bytes=48 * MIB),
        name="attention",
    )(strip, received)


def route_kernel(routes_ref, routes_t_ref, weights_ref, spread_ref, combine_ref):
    routes, routes_t, weights = routes_ref[...], routes_t_ref[...], weights_ref[...]
    expert = lax.broadcasted_iota(jnp.int32, (TOK, EXPERTS), 1)
    expert_t = lax.broadcasted_iota(jnp.int32, (EXPERTS, TOK), 0)
    named = jnp.zeros((TOK, EXPERTS), F32)
    named_t = jnp.zeros((EXPERTS, TOK), F32)
    scale = jnp.zeros((TOK, EXPERTS), F32)
    for k in range(8):
        hit = routes[:, k : k + 1] == expert
        named = jnp.where(hit, 1.0, named)
        scale = jnp.where(hit, weights[:, k : k + 1], scale)
        named_t = jnp.where(routes_t[k : k + 1, :] == expert_t, 1.0, named_t)
    row = lax.broadcasted_iota(jnp.int32, (TOK, TOK), 0)
    col = lax.broadcasted_iota(jnp.int32, (TOK, TOK), 1)
    before = jnp.where(col < row, 1.0, 0.0).astype(BF16)
    before_t = jnp.where(row < col, 1.0, 0.0).astype(BF16)
    slot = jnp.where(named > 0.5, dot_nn(before, named.astype(BF16)), -1.0).astype(BF16)
    slot_t = jnp.where(named_t > 0.5, dot_nn(named_t.astype(BF16), before_t), -1.0).astype(BF16)

    r = lax.broadcasted_iota(jnp.int32, (SLOTS, EXPERTS), 0)
    e = lax.broadcasted_iota(jnp.int32, (SLOTS, EXPERTS), 1) * CAP
    owner = jnp.where((r >= e) & (r < e + CAP), 1.0, 0.0).astype(BF16)
    r = lax.broadcasted_iota(jnp.int32, (SLOTS, TOK), 0).astype(F32)
    place = r - CAP * jnp.floor((r + 0.5) * (1.0 / CAP))
    spread_ref[...] = jnp.where(dot_nn(owner, slot_t) == place, 1.0, 0.0).astype(BF16)

    r = lax.broadcasted_iota(jnp.int32, (EXPERTS, SLOTS), 1)
    e = lax.broadcasted_iota(jnp.int32, (EXPERTS, SLOTS), 0) * CAP
    owner = jnp.where((r >= e) & (r < e + CAP), 1.0, 0.0).astype(BF16)
    r = lax.broadcasted_iota(jnp.int32, (TOK, SLOTS), 1).astype(F32)
    place = r - CAP * jnp.floor((r + 0.5) * (1.0 / CAP))
    chosen = dot_nn(slot, owner) == place
    high = scale.astype(BF16)
    low = (scale - high.astype(F32)).astype(BF16)
    combine_ref[:TOK] = jnp.where(chosen, dot_nn(high, owner), 0.0).astype(BF16)
    combine_ref[TOK:] = jnp.where(chosen, dot_nn(low, owner), 0.0).astype(BF16)


def route(routes, weights):
    return pl.pallas_call(
        route_kernel,
        out_shape=(
            jax.ShapeDtypeStruct((SLOTS, TOK), BF16),
            jax.ShapeDtypeStruct((2 * TOK, SLOTS), BF16),
        ),
        compiler_params=pltpu.CompilerParams(vmem_limit_bytes=32 * MIB),
        name="route",
    )(routes, routes.T, weights)


EXP_STEP = 8
SPREAD_ROWS = EXP_STEP * CAP


def post_kernel(x_ref, w_ref, resid_ref, gain_ref, spread_ref, mid_ref, out_ref, att_ref, norm_ref):
    @pl.when(pl.program_id(0) == 0)
    def _():
        left = left_lanes((PARTS, HALF, 128))
        for pair in range(HEADS // 2):
            pieces = []
            for head in (2 * pair, 2 * pair + 1):
                kv, group = head // GROUP, head % GROUP
                pieces.append(
                    x_ref[kv * PARTS : (kv + 1) * PARTS, group * HALF : (group + 1) * HALF, :]
                )
            even, odd = pieces
            top = jnp.where(left, even, swap_halves(odd))
            bottom = jnp.where(left, swap_halves(even), odd)
            both = jnp.concatenate([top[:, None], bottom[:, None]], axis=1)
            att_ref[:, pair * 128 : pair * 128 + 128] = both.reshape(TOK, 128)
        middle = (resid_ref[...].astype(F32) + dot_nn(att_ref[...], w_ref[...])).astype(BF16)
        mid_ref[...] = middle
        values = middle.astype(F32)
        mean_square = jnp.mean(values * values, axis=-1, keepdims=True)
        norm_ref[...] = (values * lax.rsqrt(mean_square + EPSILON) * gain_ref[...]).astype(BF16)

    out_ref[...] = dot_nn(spread_ref[...], norm_ref[...]).astype(BF16)


def post(received, weight, resid, gain, spread):
    steps = EXPERTS // EXP_STEP
    return pl.pallas_call(
        post_kernel,
        grid=(steps,),
        out_shape=(
            jax.ShapeDtypeStruct((TOK, D), BF16),
            jax.ShapeDtypeStruct((SLOTS, D), BF16),
        ),
        in_specs=[
            pl.BlockSpec((SEQ, QROWS, 128), lambda i: (0, 0, 0)),
            pl.BlockSpec((D, D), lambda i: (0, 0)),
            pl.BlockSpec((TOK, D), lambda i: (0, 0)),
            pl.BlockSpec((1, D), lambda i: (0, 0)),
            pl.BlockSpec((SPREAD_ROWS, TOK), lambda i: (i, 0)),
        ],
        out_specs=(
            pl.BlockSpec((TOK, D), lambda i: (0, 0)),
            pl.BlockSpec((SPREAD_ROWS, D), lambda i: (i, 0)),
        ),
        scratch_shapes=[pltpu.VMEM((TOK, D), BF16), pltpu.VMEM((TOK, D), BF16)],
        compiler_params=pltpu.CompilerParams(vmem_limit_bytes=48 * MIB),
        name="post",
    )(received, weight, resid, gain, spread)


EROWS = 256


def expert_kernel(x_ref, gate_ref, up_ref, down_ref, o_ref):
    rows = x_ref[...]
    gate = dot_nn(rows, gate_ref[...])
    up = dot_nn(rows, up_ref[...])
    hidden = (gate / (1.0 + jnp.exp(-gate)) * up).astype(BF16)
    o_ref[...] = dot_nn(hidden, down_ref[...]).astype(BF16)


def expert(rows, gate, up, down):
    return pl.pallas_call(
        expert_kernel,
        grid=(rows.shape[0] // EROWS,),
        out_shape=jax.ShapeDtypeStruct(rows.shape, BF16),
        in_specs=[
            pl.BlockSpec((EROWS, D), lambda i: (i, 0)),
            pl.BlockSpec((D, FFE), lambda i: (0, 0)),
            pl.BlockSpec((D, FFE), lambda i: (0, 0)),
            pl.BlockSpec((FFE, D), lambda i: (0, 0)),
        ],
        out_specs=pl.BlockSpec((EROWS, D), lambda i: (i, 0)),
        compiler_params=pltpu.CompilerParams(vmem_limit_bytes=48 * MIB),
        name="expert",
    )(rows, gate, up, down)


CCOLS = 512


def combine_kernel(c_ref, x_ref, mid_ref, o_ref):
    both = dot_nn(c_ref[...], x_ref[...])
    o_ref[...] = (mid_ref[...].astype(F32) + (both[:TOK] + both[TOK:])).astype(BF16)


def combine(matrix, rows, middle):
    return pl.pallas_call(
        combine_kernel,
        grid=(D // CCOLS,),
        out_shape=jax.ShapeDtypeStruct((TOK, D), BF16),
        in_specs=[
            pl.BlockSpec((2 * TOK, SLOTS), lambda i: (0, 0)),
            pl.BlockSpec((SLOTS, CCOLS), lambda i: (0, i)),
            pl.BlockSpec((TOK, CCOLS), lambda i: (0, i)),
        ],
        out_specs=pl.BlockSpec((TOK, CCOLS), lambda i: (0, i)),
        compiler_params=pltpu.CompilerParams(vmem_limit_bytes=48 * MIB),
        name="combine",
    )(matrix, rows, middle)


DROWS = KVH * 8


def decode_kernel(info_ref, q_ref, kn_ref, vn_ref, k_ref, v_ref, o_ref):
    request = pl.program_id(0)
    seq = info_ref[0]
    length = info_ref[1 + request]
    query = q_ref[0]
    position = seq * CBLK + lax.broadcasted_iota(jnp.int32, (DROWS, CBLK), 1)
    visible = position < length
    scores = jnp.where(visible, dot_nt(query, k_ref[0]) * SCALE, NEGATIVE)
    first = jnp.where(seq == 0, 1.0, 0.0)
    product = query.astype(F32) * kn_ref[0].astype(F32)
    fresh = jnp.sum(product, axis=1, keepdims=True) * SCALE
    fresh = jnp.where(first > 0.5, fresh, NEGATIVE)
    top = jnp.maximum(jnp.max(scores, axis=1, keepdims=True), fresh)
    weights = jnp.where(visible, jnp.exp(scores - top), 0.0)
    fresh_weight = jnp.exp(fresh - top) * first
    total = jnp.sum(weights, axis=1, keepdims=True) + fresh_weight
    fresh_round = fresh_weight.astype(BF16).astype(F32)
    weighted = dot_nn(weights.astype(BF16), v_ref[0]) + fresh_round * vn_ref[0].astype(F32)
    lane = lax.broadcasted_iota(jnp.int32, (8, 128), 1)
    for kv in range(KVH):
        rows = slice(8 * kv, 8 * kv + 8)
        lanes = slice(128 * (kv // 2), 128 * (kv // 2) + 128)
        piece = weighted[rows, lanes]
        if kv % 2:
            piece = swap_halves(piece)
        piece = jnp.where(lane < HD, piece, jnp.where(lane < 96, top[rows], total[rows]))
        o_ref[kv] = piece


def decode(info, query, key_new, value_new, key_cache, value_cache):
    return pl.pallas_call(
        decode_kernel,
        grid=(RLOC,),
        out_shape=jax.ShapeDtypeStruct((SEQ, 8, 128), F32),
        in_specs=[
            pl.BlockSpec(memory_space=pltpu.SMEM),
            pl.BlockSpec((1, DROWS, KVH * HD), lambda i: (i, 0, 0)),
            pl.BlockSpec((1, 1, KVH * HD), lambda i: (i, 0, 0)),
            pl.BlockSpec((1, 1, KVH * HD), lambda i: (i, 0, 0)),
            pl.BlockSpec((1, CBLK, KVH * HD), lambda i: (i, 0, 0)),
            pl.BlockSpec((1, CBLK, KVH * HD), lambda i: (i, 0, 0)),
        ],
        out_specs=pl.BlockSpec((KVH, 8, 128), lambda i: (i, 0, 0)),
        compiler_params=pltpu.CompilerParams(vmem_limit_bytes=48 * MIB),
        name="decode",
    )(info, query, key_new, value_new, key_cache, value_cache)


def exchange(x):
    return lax.all_to_all(x, "seq", split_axis=0, concat_axis=0, tiled=True)


def gather_req(shard, axis):
    index = lax.axis_index("req")
    across = lax.ppermute(shard, "req", [(i, i ^ 2) for i in range(4)])
    own_pair = lax.ppermute(shard, "req", [(i, i ^ 1) for i in range(4)])
    far_pair = lax.ppermute(across, "req", [(i, i ^ 1) for i in range(4)])
    size = shard.shape[axis]
    shape = list(shard.shape)
    shape[axis] = 4 * size
    full = jnp.zeros(shape, shard.dtype)
    for piece, flip in ((shard, 0), (own_pair, 1), (across, 2), (far_pair, 3)):
        full = lax.dynamic_update_slice_in_dim(full, piece, (index ^ flip) * size, axis)
    return full


def block_query(dec_query):
    rows = dec_query.reshape(RLOC, KVH, GROUP, HD)
    rows = jnp.pad(rows, ((0, 0), (0, 0), (0, 8 - GROUP), (0, 0)))
    same = jnp.eye(KVH, dtype=BF16)[None, :, None, :, None]
    return (rows[:, :, :, None, :] * same).reshape(RLOC, DROWS, KVH * HD)


def body(
    prefill_query,
    prefill_key,
    prefill_value,
    prefill_resid,
    dec_query,
    dec_key_new,
    dec_value_new,
    dec_resid,
    cache_lengths,
    key_cache,
    value_cache,
    attn_out_weight,
    ffn_gain,
    expert_gate,
    expert_up,
    expert_down,
    routes,
    route_weights,
):
    seq = lax.axis_index("seq").astype(jnp.int32)
    strip = (seq % PARTS).reshape(1)
    received = exchange(pack(prefill_query, prefill_key, prefill_value))
    gate_up = jnp.concatenate([expert_gate[0], expert_up[0]], axis=1)
    gate_up = gather_req(gate_up, 0)
    gate, up = gate_up[:, :FFE], gate_up[:, FFE:]
    down = gather_req(expert_down[0], 1)
    spread, matrix = route(routes, route_weights)
    info = jnp.concatenate([seq.reshape(1), cache_lengths])
    partial = decode(
        info,
        block_query(dec_query),
        dec_key_new.reshape(RLOC, 1, KVH * HD),
        dec_value_new.reshape(RLOC, 1, KVH * HD),
        key_cache,
        value_cache,
    )
    attended = exchange(attention(strip, received))
    middle, outgoing = post(attended, attn_out_weight, prefill_resid, ffn_gain[None, :], spread)
    incoming = exchange(outgoing.reshape(EXPERTS, CAP, D)).reshape(SLOTS, D)
    result = expert(incoming, gate, up, down)
    returned = exchange(result.reshape(EXPERTS, CAP, D)).reshape(SLOTS, D)
    prefill_out = combine(matrix, returned, middle)

    parts = exchange(partial)
    tops = parts[..., HD : HD + 1]
    top = jnp.max(tops, axis=0, keepdims=True)
    merged = jnp.sum(parts * jnp.exp(tops - top), axis=0)
    decoded = (merged[:, :HD] / merged[:, 96:97]).astype(BF16)
    decoded = jnp.pad(decoded, ((0, 0), (0, 128 - HD)))
    decoded = exchange(jnp.broadcast_to(decoded[None], (SEQ, 8, 128)))
    decoded = decoded[:, :GROUP, :HD].reshape(RLOC, HEADS * HD)
    dec_out = (
        dec_resid.astype(F32) + jnp.dot(decoded, attn_out_weight, preferred_element_type=F32)
    ).astype(BF16)
    return (prefill_out, dec_out)


def solution(mesh):
    return jax.shard_map(
        body,
        mesh=mesh,
        in_specs=(
            P(("req", "seq"), None),
            P(("req", "seq"), None),
            P(("req", "seq"), None),
            P(("req", "seq"), None),
            P("req", None),
            P("req", None),
            P("req", None),
            P("req", None),
            P("req"),
            P("req", "seq", None),
            P("req", "seq", None),
            P(),
            P(),
            P("seq", "req", None),
            P("seq", "req", None),
            P("seq", None, "req"),
            P(("req", "seq"), None),
            P(("req", "seq"), None),
        ),
        out_specs=(P(("req", "seq"), None), P("req", None)),
        check_vma=False,
    )
```

```python
import jax
import jax.numpy as jnp
from jax import lax
from jax.experimental import pallas as pl
from jax.experimental.pallas import tpu as pltpu
from jax.sharding import PartitionSpec as P

D = 1536
HEADS = 24
KVH = 8
GROUP = HEADS // KVH
HD = 64
FFE = 512
EXPERTS = 32
CAP = 40
TOK = 128
SEQ = 32
PARTS = SEQ // KVH
STRIP = TOK // PARTS
HALF = STRIP // 2
QROWS = GROUP * HALF
PACK = TOK + QROWS
BACK = QROWS + 8
SLOTS = EXPERTS * CAP
CBLK = 1024
RLOC = 4

NEGATIVE = -1e30
EPSILON = 1e-05
SCALE = 0.125
F32 = jnp.float32
BF16 = jnp.bfloat16
MIB = 1 << 20


def swap_halves(x):
    return jnp.concatenate([x[..., HD:], x[..., :HD]], axis=-1)


def left_lanes(shape):
    return lax.broadcasted_iota(jnp.int32, shape, len(shape) - 1) < HD


def dot_nt(a, b):
    return lax.dot_general(a, b, (((1,), (1,)), ((), ())), preferred_element_type=F32)


def dot_nn(a, b):
    return lax.dot_general(a, b, (((1,), (0,)), ((), ())), preferred_element_type=F32)


PACK_STEPS = 4
PAIRS = HEADS // 2 // PACK_STEPS


def pack_kernel(q_ref, k_ref, v_ref, o_ref):
    left = left_lanes((TOK, 2 * HD))
    keys, values = k_ref[...], v_ref[...]
    even = jnp.where(left, keys, swap_halves(values))
    odd = jnp.where(left, swap_halves(keys), values)
    for part in range(PARTS):
        o_ref[part, :TOK, :] = even
        o_ref[PARTS + part, :TOK, :] = odd
    left = left_lanes((PARTS * HALF, 2 * HD))
    for pair in range(PAIRS):
        rows = q_ref[:, pair * 128 : pair * 128 + 128] * jnp.asarray(SCALE, BF16)
        rows = rows.reshape(PARTS, 2, HALF, 128)
        top = rows[:, 0].reshape(PARTS * HALF, 128)
        bottom = rows[:, 1].reshape(PARTS * HALF, 128)
        even = jnp.where(left, top, swap_halves(bottom))
        odd = jnp.where(left, swap_halves(top), bottom)
        for head, packed in ((2 * pair, even), (2 * pair + 1, odd)):
            kv, group = head // GROUP, head % GROUP
            for part in range(PARTS):
                o_ref[
                    kv * PARTS + part, TOK + group * HALF : TOK + (group + 1) * HALF, :
                ] = packed[part * HALF : (part + 1) * HALF]


def pack(query, key, value):
    return pl.pallas_call(
        pack_kernel,
        grid=(PACK_STEPS,),
        out_shape=jax.ShapeDtypeStruct((SEQ, PACK, 128), BF16),
        in_specs=[
            pl.BlockSpec((TOK, PAIRS * 128), lambda i: (0, i)),
            pl.BlockSpec((TOK, 128), lambda i: (0, i)),
            pl.BlockSpec((TOK, 128), lambda i: (0, i)),
        ],
        out_specs=pl.BlockSpec((SEQ // PACK_STEPS, PACK, 128), lambda i: (i, 0, 0)),
        compiler_params=pltpu.CompilerParams(vmem_limit_bytes=32 * MIB),
        name="pack",
    )(query, key, value)


QS = 8
KS = 8
TILE = QS * 2 * QROWS
KBLK = KS * TOK


def attention_kernel(strip_ref, x_ref, dec_ref, o_ref, ones_ref, q_ref, m_ref, acc_ref):
    strip = strip_ref[0]
    o_ref[:, QROWS:, :] = dec_ref[...]
    for block in range(SEQ // KS):
        kv = x_ref[block * KS : (block + 1) * KS, :TOK, :].reshape(KBLK, 128)
        ones_ref[block] = jnp.where(left_lanes((KBLK, 128)), jnp.asarray(1.0, BF16), kv)
    half = QS * QROWS
    left = left_lanes((half, 128))
    row = lax.broadcasted_iota(jnp.int32, (TILE, KBLK), 0)
    lower = row >= half
    row = jnp.where(lower, row - half, row)
    source = row // QROWS
    inner = row % HALF
    position = source * TOK + strip * STRIP + inner + jnp.where(lower, HALF, 0)
    key_position = lax.broadcasted_iota(jnp.int32, (TILE, KBLK), 1)
    visible = key_position <= position

    def step(block, masked):
        kv = x_ref[pl.ds(block * KS, KS), :TOK, :].reshape(KBLK, 128)
        scores = dot_nt(q_ref[...], kv)
        if masked:
            scores = jnp.where(visible, scores, NEGATIVE)
        before = m_ref[...]
        top = jnp.maximum(before, jnp.max(scores, axis=1, keepdims=True))
        weights = jnp.exp(scores - top[:, :1]).astype(BF16)
        acc_ref[...] = acc_ref[...] * jnp.exp(before - top) + dot_nn(weights, ones_ref[block])
        m_ref[...] = top

    def tile(number, carry):
        packed = x_ref[pl.ds(number * QS, QS), TOK:, :].reshape(half, 128)
        zero = jnp.zeros_like(packed)
        q_ref[:half] = jnp.where(left, packed, zero)
        q_ref[half:] = jnp.where(left, swap_halves(packed), zero)
        m_ref[...] = jnp.full((TILE, 128), NEGATIVE, F32)
        acc_ref[...] = jnp.zeros((TILE, 128), F32)

        def block(index, inner_carry):
            step(index, False)
            return inner_carry

        lax.fori_loop(0, number, block, 0)
        step(number, True)
        total = acc_ref[...]
        result = total / swap_halves(total)
        merged = jnp.where(left, swap_halves(result[:half]), result[half:])
        o_ref[pl.ds(number * QS, QS), :QROWS, :] = merged.astype(BF16).reshape(QS, QROWS, 128)
        return carry

    lax.fori_loop(0, SEQ // QS, tile, 0)


def attention(strip, received, partial):
    return pl.pallas_call(
        attention_kernel,
        out_shape=jax.ShapeDtypeStruct((SEQ, BACK, 128), BF16),
        in_specs=[
            pl.BlockSpec(memory_space=pltpu.SMEM),
            pl.BlockSpec(memory_space=pltpu.VMEM),
            pl.BlockSpec(memory_space=pltpu.VMEM),
        ],
        scratch_shapes=[
            pltpu.VMEM((SEQ // KS, KBLK, 128), BF16),
            pltpu.VMEM((TILE, 128), BF16),
            pltpu.VMEM((TILE, 128), F32),
            pltpu.VMEM((TILE, 128), F32),
        ],
        compiler_params=pltpu.CompilerParams(vmem_limit_bytes=48 * MIB),
        name="attention",
    )(strip, received, partial)


def route_kernel(routes_ref, routes_t_ref, weights_ref, spread_ref, combine_ref):
    routes, routes_t, weights = routes_ref[...], routes_t_ref[...], weights_ref[...]
    expert = lax.broadcasted_iota(jnp.int32, (TOK, EXPERTS), 1)
    expert_t = lax.broadcasted_iota(jnp.int32, (EXPERTS, TOK), 0)
    named = jnp.zeros((TOK, EXPERTS), F32)
    named_t = jnp.zeros((EXPERTS, TOK), F32)
    scale = jnp.zeros((TOK, EXPERTS), F32)
    for k in range(8):
        hit = routes[:, k : k + 1] == expert
        named = jnp.where(hit, 1.0, named)
        scale = jnp.where(hit, weights[:, k : k + 1], scale)
        named_t = jnp.where(routes_t[k : k + 1, :] == expert_t, 1.0, named_t)
    row = lax.broadcasted_iota(jnp.int32, (TOK, TOK), 0)
    col = lax.broadcasted_iota(jnp.int32, (TOK, TOK), 1)
    before = jnp.where(col < row, 1.0, 0.0).astype(BF16)
    before_t = jnp.where(row < col, 1.0, 0.0).astype(BF16)
    slot = jnp.where(named > 0.5, dot_nn(before, named.astype(BF16)), -1.0).astype(BF16)
    slot_t = jnp.where(named_t > 0.5, dot_nn(named_t.astype(BF16), before_t), -1.0).astype(BF16)

    r = lax.broadcasted_iota(jnp.int32, (SLOTS, EXPERTS), 0)
    e = lax.broadcasted_iota(jnp.int32, (SLOTS, EXPERTS), 1) * CAP
    owner = jnp.where((r >= e) & (r < e + CAP), 1.0, 0.0).astype(BF16)
    r = lax.broadcasted_iota(jnp.int32, (SLOTS, TOK), 0).astype(F32)
    place = r - CAP * jnp.floor((r + 0.5) * (1.0 / CAP))
    spread_ref[...] = jnp.where(dot_nn(owner, slot_t) == place, 1.0, 0.0).astype(BF16)

    r = lax.broadcasted_iota(jnp.int32, (EXPERTS, SLOTS), 1)
    e = lax.broadcasted_iota(jnp.int32, (EXPERTS, SLOTS), 0) * CAP
    owner = jnp.where((r >= e) & (r < e + CAP), 1.0, 0.0).astype(BF16)
    r = lax.broadcasted_iota(jnp.int32, (TOK, SLOTS), 1).astype(F32)
    place = r - CAP * jnp.floor((r + 0.5) * (1.0 / CAP))
    chosen = dot_nn(slot, owner) == place
    high = scale.astype(BF16)
    low = (scale - high.astype(F32)).astype(BF16)
    combine_ref[:TOK] = jnp.where(chosen, dot_nn(high, owner), 0.0).astype(BF16)
    combine_ref[TOK:] = jnp.where(chosen, dot_nn(low, owner), 0.0).astype(BF16)


def route(routes, weights):
    return pl.pallas_call(
        route_kernel,
        out_shape=(
            jax.ShapeDtypeStruct((SLOTS, TOK), BF16),
            jax.ShapeDtypeStruct((2 * TOK, SLOTS), BF16),
        ),
        compiler_params=pltpu.CompilerParams(vmem_limit_bytes=32 * MIB),
        name="route",
    )(routes, routes.T, weights)


EXP_STEP = 8
SPREAD_ROWS = EXP_STEP * CAP


def post_kernel(x_ref, w_ref, resid_ref, gain_ref, spread_ref, mid_ref, out_ref, att_ref, norm_ref):
    @pl.when(pl.program_id(0) == 0)
    def _():
        left = left_lanes((PARTS, HALF, 128))
        for pair in range(HEADS // 2):
            pieces = []
            for head in (2 * pair, 2 * pair + 1):
                kv, group = head // GROUP, head % GROUP
                pieces.append(
                    x_ref[kv * PARTS : (kv + 1) * PARTS, group * HALF : (group + 1) * HALF, :]
                )
            even, odd = pieces
            top = jnp.where(left, even, swap_halves(odd))
            bottom = jnp.where(left, swap_halves(even), odd)
            both = jnp.concatenate([top[:, None], bottom[:, None]], axis=1)
            att_ref[:, pair * 128 : pair * 128 + 128] = both.reshape(TOK, 128)
        middle = (resid_ref[...].astype(F32) + dot_nn(att_ref[...], w_ref[...])).astype(BF16)
        mid_ref[...] = middle
        values = middle.astype(F32)
        mean_square = jnp.mean(values * values, axis=-1, keepdims=True)
        norm_ref[...] = (values * lax.rsqrt(mean_square + EPSILON) * gain_ref[...]).astype(BF16)

    out_ref[...] = dot_nn(spread_ref[...], norm_ref[...]).astype(BF16)


def post(received, weight, resid, gain, spread):
    steps = EXPERTS // EXP_STEP
    return pl.pallas_call(
        post_kernel,
        grid=(steps,),
        out_shape=(
            jax.ShapeDtypeStruct((TOK, D), BF16),
            jax.ShapeDtypeStruct((SLOTS, D), BF16),
        ),
        in_specs=[
            pl.BlockSpec((SEQ, BACK, 128), lambda i: (0, 0, 0)),
            pl.BlockSpec((D, D), lambda i: (0, 0)),
            pl.BlockSpec((TOK, D), lambda i: (0, 0)),
            pl.BlockSpec((1, D), lambda i: (0, 0)),
            pl.BlockSpec((SPREAD_ROWS, TOK), lambda i: (i, 0)),
        ],
        out_specs=(
            pl.BlockSpec((TOK, D), lambda i: (0, 0)),
            pl.BlockSpec((SPREAD_ROWS, D), lambda i: (i, 0)),
        ),
        scratch_shapes=[pltpu.VMEM((TOK, D), BF16), pltpu.VMEM((TOK, D), BF16)],
        compiler_params=pltpu.CompilerParams(vmem_limit_bytes=48 * MIB),
        name="post",
    )(received, weight, resid, gain, spread)


EROWS = 256


def expert_kernel(x_ref, w_ref, o_ref):
    both = dot_nn(x_ref[...], w_ref[:, : 2 * FFE])
    gate, up = both[:, :FFE], both[:, FFE:]
    hidden = (gate / (1.0 + jnp.exp(-gate)) * up).astype(BF16)
    o_ref[...] = dot_nt(hidden, w_ref[:, 2 * FFE :]).astype(BF16)


def expert(rows, weights):
    return pl.pallas_call(
        expert_kernel,
        grid=(rows.shape[0] // EROWS,),
        out_shape=jax.ShapeDtypeStruct(rows.shape, BF16),
        in_specs=[
            pl.BlockSpec((EROWS, D), lambda i: (i, 0)),
            pl.BlockSpec((D, 3 * FFE), lambda i: (0, 0)),
        ],
        out_specs=pl.BlockSpec((EROWS, D), lambda i: (i, 0)),
        compiler_params=pltpu.CompilerParams(vmem_limit_bytes=48 * MIB),
        name="expert",
    )(rows, weights)


CCOLS = 512


def combine_kernel(c_ref, x_ref, mid_ref, o_ref):
    both = dot_nn(c_ref[...], x_ref[...])
    o_ref[...] = (mid_ref[...].astype(F32) + (both[:TOK] + both[TOK:])).astype(BF16)


def combine(matrix, rows, middle):
    return pl.pallas_call(
        combine_kernel,
        grid=(D // CCOLS,),
        out_shape=jax.ShapeDtypeStruct((TOK, D), BF16),
        in_specs=[
            pl.BlockSpec((2 * TOK, SLOTS), lambda i: (0, 0)),
            pl.BlockSpec((SLOTS, CCOLS), lambda i: (0, i)),
            pl.BlockSpec((TOK, CCOLS), lambda i: (0, i)),
        ],
        out_specs=pl.BlockSpec((TOK, CCOLS), lambda i: (0, i)),
        compiler_params=pltpu.CompilerParams(vmem_limit_bytes=48 * MIB),
        name="combine",
    )(matrix, rows, middle)


DROWS = KVH * 8


def pieces_of(x, count):
    pieces = []
    for _ in range(count):
        piece = x.astype(BF16).astype(F32)
        pieces.append(piece)
        x = x - piece
    return pieces


def decode_kernel(info_ref, q_ref, kn_ref, vn_ref, k_ref, v_ref, o_ref):
    request = pl.program_id(0)
    seq = info_ref[0]
    length = info_ref[1 + request]
    query = q_ref[0]
    position = seq * CBLK + lax.broadcasted_iota(jnp.int32, (DROWS, CBLK), 1)
    visible = position < length
    scores = jnp.where(visible, dot_nt(query, k_ref[0]) * SCALE, NEGATIVE)
    first = jnp.where(seq == 0, 1.0, 0.0)
    product = query.astype(F32) * kn_ref[0].astype(F32)
    fresh = jnp.sum(product, axis=1, keepdims=True) * SCALE
    fresh = jnp.where(first > 0.5, fresh, NEGATIVE)
    top = jnp.maximum(jnp.max(scores, axis=1, keepdims=True), fresh)
    weights = jnp.where(visible, jnp.exp(scores - top), 0.0)
    fresh_weight = jnp.exp(fresh - top) * first
    total = jnp.sum(weights, axis=1, keepdims=True) + fresh_weight
    fresh_round = fresh_weight.astype(BF16).astype(F32)
    weighted = dot_nn(weights.astype(BF16), v_ref[0]) + fresh_round * vn_ref[0].astype(F32)
    weighted = weighted / jnp.maximum(total, 1e-30)
    stats = pieces_of(top, 3) + pieces_of(total, 3)
    lane = lax.broadcasted_iota(jnp.int32, (DROWS, 128), 1)
    packed = jnp.zeros((DROWS, 128), F32)
    for number, piece in enumerate(stats):
        packed = jnp.where(lane >= HD + 8 * number, piece, packed)
    lane = lax.broadcasted_iota(jnp.int32, (8, 128), 1)
    for kv in range(KVH):
        rows = slice(8 * kv, 8 * kv + 8)
        lanes = slice(128 * (kv // 2), 128 * (kv // 2) + 128)
        piece = weighted[rows, lanes]
        if kv % 2:
            piece = swap_halves(piece)
        o_ref[kv] = jnp.where(lane < HD, piece, packed[rows]).astype(BF16)


def decode(info, query, key_new, value_new, key_cache, value_cache):
    return pl.pallas_call(
        decode_kernel,
        grid=(RLOC,),
        out_shape=jax.ShapeDtypeStruct((SEQ, 8, 128), BF16),
        in_specs=[
            pl.BlockSpec(memory_space=pltpu.SMEM),
            pl.BlockSpec((1, DROWS, KVH * HD), lambda i: (i, 0, 0)),
            pl.BlockSpec((1, 1, KVH * HD), lambda i: (i, 0, 0)),
            pl.BlockSpec((1, 1, KVH * HD), lambda i: (i, 0, 0)),
            pl.BlockSpec((1, CBLK, KVH * HD), lambda i: (i, 0, 0)),
            pl.BlockSpec((1, CBLK, KVH * HD), lambda i: (i, 0, 0)),
        ],
        out_specs=pl.BlockSpec((KVH, 8, 128), lambda i: (i, 0, 0)),
        compiler_params=pltpu.CompilerParams(vmem_limit_bytes=48 * MIB),
        name="decode",
    )(info, query, key_new, value_new, key_cache, value_cache)


def exchange(x):
    return lax.all_to_all(x, "seq", split_axis=0, concat_axis=0, tiled=True)


def join_req(own, pair, far, far_pair):
    index = lax.axis_index("req")
    size = own.shape[0]
    full = jnp.zeros((4 * size, own.shape[1]), own.dtype)
    for piece, flip in ((own, 0), (pair, 1), (far, 2), (far_pair, 3)):
        full = lax.dynamic_update_slice_in_dim(full, piece, (index ^ flip) * size, 0)
    return full


def merge_decode(tails):
    values = tails.astype(F32)
    stats = values[:, :, HD : HD + 48].reshape(SEQ, 8, 6, 8)[..., 0]
    tops = jnp.sum(stats[..., :3], axis=-1, keepdims=True)
    totals = jnp.sum(stats[..., 3:], axis=-1, keepdims=True)
    weights = totals * jnp.exp(tops - jnp.max(tops, axis=0, keepdims=True))
    merged = jnp.sum(values[:, :, :HD] * weights, axis=0) / jnp.sum(weights, axis=0)
    merged = jnp.pad(merged.astype(BF16), ((0, 0), (0, 128 - HD)))
    return jnp.broadcast_to(merged[None], (SEQ, 8, 128))


def block_query(dec_query):
    rows = dec_query.reshape(RLOC, KVH, GROUP, HD)
    rows = jnp.pad(rows, ((0, 0), (0, 0), (0, 8 - GROUP), (0, 0)))
    same = jnp.eye(KVH, dtype=BF16)[None, :, None, :, None]
    return (rows[:, :, :, None, :] * same).reshape(RLOC, DROWS, KVH * HD)


def body(
    prefill_query,
    prefill_key,
    prefill_value,
    prefill_resid,
    dec_query,
    dec_key_new,
    dec_value_new,
    dec_resid,
    cache_lengths,
    key_cache,
    value_cache,
    attn_out_weight,
    ffn_gain,
    expert_gate,
    expert_up,
    expert_down,
    routes,
    route_weights,
):
    seq = lax.axis_index("seq").astype(jnp.int32)
    strip = (seq % PARTS).reshape(1)
    own = jnp.concatenate([expert_gate[0], expert_up[0], expert_down[0].T], axis=1)
    near = [(i, i ^ 1) for i in range(4)]
    far = lax.ppermute(own, "req", [(i, i ^ 2) for i in range(4)])
    received = exchange(pack(prefill_query, prefill_key, prefill_value))
    spread, matrix = route(routes, route_weights)
    info = jnp.concatenate([seq.reshape(1), cache_lengths])
    partial = decode(
        info,
        block_query(dec_query),
        dec_key_new.reshape(RLOC, 1, KVH * HD),
        dec_value_new.reshape(RLOC, 1, KVH * HD),
        key_cache,
        value_cache,
    )
    received, partial, spread, matrix = lax.optimization_barrier(
        (received, partial, spread, matrix)
    )
    attended = exchange(attention(strip, received, partial))
    attended, far = lax.optimization_barrier((attended, far))
    middle, outgoing = post(attended, attn_out_weight, prefill_resid, ffn_gain[None, :], spread)
    outgoing, far, own = lax.optimization_barrier((outgoing, far, own))
    incoming = exchange(outgoing.reshape(EXPERTS, CAP, D)).reshape(SLOTS, D)
    weights = join_req(own, lax.ppermute(own, "req", near), far, lax.ppermute(far, "req", near))
    incoming, weights = lax.optimization_barrier((incoming, weights))
    result = expert(incoming, weights)
    result, tails = lax.optimization_barrier((result, attended[:, QROWS:, :]))
    returned = exchange(result.reshape(EXPERTS, CAP, D)).reshape(SLOTS, D)
    decoded = exchange(merge_decode(tails))
    decoded = decoded[:, :GROUP, :HD].reshape(RLOC, HEADS * HD)
    dec_out = (
        dec_resid.astype(F32) + jnp.dot(decoded, attn_out_weight, preferred_element_type=F32)
    ).astype(BF16)
    prefill_out = combine(matrix, returned, middle)
    return (prefill_out, dec_out)


def solution(mesh):
    return jax.shard_map(
        body,
        mesh=mesh,
        in_specs=(
            P(("req", "seq"), None),
            P(("req", "seq"), None),
            P(("req", "seq"), None),
            P(("req", "seq"), None),
            P("req", None),
            P("req", None),
            P("req", None),
            P("req", None),
            P("req"),
            P("req", "seq", None),
            P("req", "seq", None),
            P(),
            P(),
            P("seq", "req", None),
            P("seq", "req", None),
            P("seq", None, "req"),
            P(("req", "seq"), None),
            P(("req", "seq"), None),
        ),
        out_specs=(P(("req", "seq"), None), P("req", None)),
        check_vma=False,
    )
```

```python
import jax
import jax.numpy as jnp
from jax import lax
from jax.experimental import pallas as pl
from jax.experimental.pallas import tpu as pltpu
from jax.sharding import PartitionSpec as P

D = 1536
HEADS = 24
KVH = 8
GROUP = HEADS // KVH
HD = 64
FFE = 512
EXPERTS = 32
CAP = 40
TOK = 128
SEQ = 32
PARTS = SEQ // KVH
STRIP = TOK // PARTS
HALF = STRIP // 2
QROWS = GROUP * HALF
PACK = TOK + QROWS
BACK = QROWS + 8
SLOTS = EXPERTS * CAP
CBLK = 1024
RLOC = 4

NEGATIVE = -1e30
EPSILON = 1e-05
SCALE = 0.125
F32 = jnp.float32
BF16 = jnp.bfloat16
MIB = 1 << 20


def swap_halves(x):
    return jnp.concatenate([x[..., HD:], x[..., :HD]], axis=-1)


def left_lanes(shape):
    return lax.broadcasted_iota(jnp.int32, shape, len(shape) - 1) < HD


def in_hbm(x):
    return pltpu.with_memory_space_constraint(x, pltpu.HBM)


def dot_nt(a, b):
    return lax.dot_general(a, b, (((1,), (1,)), ((), ())), preferred_element_type=F32)


def dot_nn(a, b):
    return lax.dot_general(a, b, (((1,), (0,)), ((), ())), preferred_element_type=F32)


PACK_STEPS = 4
PAIRS = HEADS // 2 // PACK_STEPS


def pack_kernel(q_ref, k_ref, v_ref, o_ref):
    left = left_lanes((TOK, 2 * HD))
    keys, values = k_ref[...], v_ref[...]
    even = jnp.where(left, keys, swap_halves(values))
    odd = jnp.where(left, swap_halves(keys), values)
    for part in range(PARTS):
        o_ref[part, :TOK, :] = even
        o_ref[PARTS + part, :TOK, :] = odd
    left = left_lanes((PARTS * HALF, 2 * HD))
    for pair in range(PAIRS):
        rows = q_ref[:, pair * 128 : pair * 128 + 128] * jnp.asarray(SCALE, BF16)
        rows = rows.reshape(PARTS, 2, HALF, 128)
        top = rows[:, 0].reshape(PARTS * HALF, 128)
        bottom = rows[:, 1].reshape(PARTS * HALF, 128)
        even = jnp.where(left, top, swap_halves(bottom))
        odd = jnp.where(left, swap_halves(top), bottom)
        for head, packed in ((2 * pair, even), (2 * pair + 1, odd)):
            kv, group = head // GROUP, head % GROUP
            for part in range(PARTS):
                o_ref[
                    kv * PARTS + part, TOK + group * HALF : TOK + (group + 1) * HALF, :
                ] = packed[part * HALF : (part + 1) * HALF]


def pack(query, key, value):
    return pl.pallas_call(
        pack_kernel,
        grid=(PACK_STEPS,),
        out_shape=pltpu.HBM((SEQ, PACK, 128), BF16),
        in_specs=[
            pl.BlockSpec((TOK, PAIRS * 128), lambda i: (0, i)),
            pl.BlockSpec((TOK, 128), lambda i: (0, i)),
            pl.BlockSpec((TOK, 128), lambda i: (0, i)),
        ],
        out_specs=pl.BlockSpec((SEQ // PACK_STEPS, PACK, 128), lambda i: (i, 0, 0)),
        compiler_params=pltpu.CompilerParams(vmem_limit_bytes=32 * MIB),
        name="pack",
    )(in_hbm(query), in_hbm(key), in_hbm(value))


QS = 8
KS = 8
TILE = QS * 2 * QROWS
KBLK = KS * TOK


def attention_kernel(strip_ref, x_ref, dec_ref, o_ref, ones_ref, q_ref, m_ref, acc_ref):
    strip = strip_ref[0]
    o_ref[:, QROWS:, :] = dec_ref[...]
    for block in range(SEQ // KS):
        kv = x_ref[block * KS : (block + 1) * KS, :TOK, :].reshape(KBLK, 128)
        ones_ref[block] = jnp.where(left_lanes((KBLK, 128)), jnp.asarray(1.0, BF16), kv)
    half = QS * QROWS
    left = left_lanes((half, 128))
    row = lax.broadcasted_iota(jnp.int32, (TILE, KBLK), 0)
    lower = row >= half
    row = jnp.where(lower, row - half, row)
    source = row // QROWS
    inner = row % HALF
    position = source * TOK + strip * STRIP + inner + jnp.where(lower, HALF, 0)
    key_position = lax.broadcasted_iota(jnp.int32, (TILE, KBLK), 1)
    visible = key_position <= position

    def step(block, masked):
        kv = x_ref[pl.ds(block * KS, KS), :TOK, :].reshape(KBLK, 128)
        scores = dot_nt(q_ref[...], kv)
        if masked:
            scores = jnp.where(visible, scores, NEGATIVE)
        before = m_ref[...]
        top = jnp.maximum(before, jnp.max(scores, axis=1, keepdims=True))
        weights = jnp.exp(scores - top[:, :1]).astype(BF16)
        acc_ref[...] = acc_ref[...] * jnp.exp(before - top) + dot_nn(weights, ones_ref[block])
        m_ref[...] = top

    def tile(number, carry):
        packed = x_ref[pl.ds(number * QS, QS), TOK:, :].reshape(half, 128)
        zero = jnp.zeros_like(packed)
        q_ref[:half] = jnp.where(left, packed, zero)
        q_ref[half:] = jnp.where(left, swap_halves(packed), zero)
        m_ref[...] = jnp.full((TILE, 128), NEGATIVE, F32)
        acc_ref[...] = jnp.zeros((TILE, 128), F32)

        def block(index, inner_carry):
            step(index, False)
            return inner_carry

        lax.fori_loop(0, number, block, 0)
        step(number, True)
        total = acc_ref[...]
        result = total / swap_halves(total)
        merged = jnp.where(left, swap_halves(result[:half]), result[half:])
        o_ref[pl.ds(number * QS, QS), :QROWS, :] = merged.astype(BF16).reshape(QS, QROWS, 128)
        return carry

    lax.fori_loop(0, SEQ // QS, tile, 0)


def attention(strip, received, partial):
    return pl.pallas_call(
        attention_kernel,
        out_shape=jax.ShapeDtypeStruct((SEQ, BACK, 128), BF16),
        in_specs=[
            pl.BlockSpec(memory_space=pltpu.SMEM),
            pl.BlockSpec(memory_space=pltpu.VMEM),
            pl.BlockSpec(memory_space=pltpu.VMEM),
        ],
        scratch_shapes=[
            pltpu.VMEM((SEQ // KS, KBLK, 128), BF16),
            pltpu.VMEM((TILE, 128), BF16),
            pltpu.VMEM((TILE, 128), F32),
            pltpu.VMEM((TILE, 128), F32),
        ],
        compiler_params=pltpu.CompilerParams(vmem_limit_bytes=48 * MIB),
        name="attention",
    )(strip, received, partial)


def route_kernel(routes_ref, routes_t_ref, weights_ref, spread_ref, combine_ref):
    routes, routes_t, weights = routes_ref[...], routes_t_ref[...], weights_ref[...]
    expert = lax.broadcasted_iota(jnp.int32, (TOK, EXPERTS), 1)
    expert_t = lax.broadcasted_iota(jnp.int32, (EXPERTS, TOK), 0)
    named = jnp.zeros((TOK, EXPERTS), F32)
    named_t = jnp.zeros((EXPERTS, TOK), F32)
    scale = jnp.zeros((TOK, EXPERTS), F32)
    for k in range(8):
        hit = routes[:, k : k + 1] == expert
        named = jnp.where(hit, 1.0, named)
        scale = jnp.where(hit, weights[:, k : k + 1], scale)
        named_t = jnp.where(routes_t[k : k + 1, :] == expert_t, 1.0, named_t)
    row = lax.broadcasted_iota(jnp.int32, (TOK, TOK), 0)
    col = lax.broadcasted_iota(jnp.int32, (TOK, TOK), 1)
    before = jnp.where(col < row, 1.0, 0.0).astype(BF16)
    before_t = jnp.where(row < col, 1.0, 0.0).astype(BF16)
    slot = jnp.where(named > 0.5, dot_nn(before, named.astype(BF16)), -1.0).astype(BF16)
    slot_t = jnp.where(named_t > 0.5, dot_nn(named_t.astype(BF16), before_t), -1.0).astype(BF16)

    r = lax.broadcasted_iota(jnp.int32, (SLOTS, EXPERTS), 0)
    e = lax.broadcasted_iota(jnp.int32, (SLOTS, EXPERTS), 1) * CAP
    owner = jnp.where((r >= e) & (r < e + CAP), 1.0, 0.0).astype(BF16)
    r = lax.broadcasted_iota(jnp.int32, (SLOTS, TOK), 0).astype(F32)
    place = r - CAP * jnp.floor((r + 0.5) * (1.0 / CAP))
    spread_ref[...] = jnp.where(dot_nn(owner, slot_t) == place, 1.0, 0.0).astype(BF16)

    r = lax.broadcasted_iota(jnp.int32, (EXPERTS, SLOTS), 1)
    e = lax.broadcasted_iota(jnp.int32, (EXPERTS, SLOTS), 0) * CAP
    owner = jnp.where((r >= e) & (r < e + CAP), 1.0, 0.0).astype(BF16)
    r = lax.broadcasted_iota(jnp.int32, (TOK, SLOTS), 1).astype(F32)
    place = r - CAP * jnp.floor((r + 0.5) * (1.0 / CAP))
    chosen = dot_nn(slot, owner) == place
    high = scale.astype(BF16)
    low = (scale - high.astype(F32)).astype(BF16)
    combine_ref[:TOK] = jnp.where(chosen, dot_nn(high, owner), 0.0).astype(BF16)
    combine_ref[TOK:] = jnp.where(chosen, dot_nn(low, owner), 0.0).astype(BF16)


def route(routes, weights):
    return pl.pallas_call(
        route_kernel,
        out_shape=(
            jax.ShapeDtypeStruct((SLOTS, TOK), BF16),
            jax.ShapeDtypeStruct((2 * TOK, SLOTS), BF16),
        ),
        compiler_params=pltpu.CompilerParams(vmem_limit_bytes=32 * MIB),
        name="route",
    )(routes, routes.T, weights)


EXP_STEP = 8
SPREAD_ROWS = EXP_STEP * CAP


def post_kernel(x_ref, w_ref, resid_ref, gain_ref, spread_ref, mid_ref, out_ref, att_ref, norm_ref):
    @pl.when(pl.program_id(0) == 0)
    def _():
        left = left_lanes((PARTS, HALF, 128))
        for pair in range(HEADS // 2):
            pieces = []
            for head in (2 * pair, 2 * pair + 1):
                kv, group = head // GROUP, head % GROUP
                pieces.append(
                    x_ref[kv * PARTS : (kv + 1) * PARTS, group * HALF : (group + 1) * HALF, :]
                )
            even, odd = pieces
            top = jnp.where(left, even, swap_halves(odd))
            bottom = jnp.where(left, swap_halves(even), odd)
            both = jnp.concatenate([top[:, None], bottom[:, None]], axis=1)
            att_ref[:, pair * 128 : pair * 128 + 128] = both.reshape(TOK, 128)
        middle = (resid_ref[...].astype(F32) + dot_nn(att_ref[...], w_ref[...])).astype(BF16)
        mid_ref[...] = middle
        values = middle.astype(F32)
        mean_square = jnp.mean(values * values, axis=-1, keepdims=True)
        norm_ref[...] = (values * lax.rsqrt(mean_square + EPSILON) * gain_ref[...]).astype(BF16)

    out_ref[...] = dot_nn(spread_ref[...], norm_ref[...]).astype(BF16)


def post(received, weight, resid, gain, spread):
    steps = EXPERTS // EXP_STEP
    return pl.pallas_call(
        post_kernel,
        grid=(steps,),
        out_shape=(
            jax.ShapeDtypeStruct((TOK, D), BF16),
            pltpu.HBM((SLOTS, D), BF16),
        ),
        in_specs=[
            pl.BlockSpec((SEQ, BACK, 128), lambda i: (0, 0, 0)),
            pl.BlockSpec((D, D), lambda i: (0, 0)),
            pl.BlockSpec((TOK, D), lambda i: (0, 0)),
            pl.BlockSpec((1, D), lambda i: (0, 0)),
            pl.BlockSpec((SPREAD_ROWS, TOK), lambda i: (i, 0)),
        ],
        out_specs=(
            pl.BlockSpec((TOK, D), lambda i: (0, 0)),
            pl.BlockSpec((SPREAD_ROWS, D), lambda i: (i, 0)),
        ),
        scratch_shapes=[pltpu.VMEM((TOK, D), BF16), pltpu.VMEM((TOK, D), BF16)],
        compiler_params=pltpu.CompilerParams(vmem_limit_bytes=48 * MIB),
        name="post",
    )(received, weight, resid, gain, spread)


EROWS = 256


def expert_kernel(x_ref, w_ref, o_ref):
    both = dot_nn(x_ref[...], w_ref[:, : 2 * FFE])
    gate, up = both[:, :FFE], both[:, FFE:]
    hidden = (gate / (1.0 + jnp.exp(-gate)) * up).astype(BF16)
    o_ref[...] = dot_nt(hidden, w_ref[:, 2 * FFE :]).astype(BF16)


def expert(rows, weights):
    return pl.pallas_call(
        expert_kernel,
        grid=(rows.shape[0] // EROWS,),
        out_shape=pltpu.HBM(rows.shape, BF16),
        in_specs=[
            pl.BlockSpec((EROWS, D), lambda i: (i, 0)),
            pl.BlockSpec((D, 3 * FFE), lambda i: (0, 0)),
        ],
        out_specs=pl.BlockSpec((EROWS, D), lambda i: (i, 0)),
        compiler_params=pltpu.CompilerParams(vmem_limit_bytes=48 * MIB),
        name="expert",
    )(rows, weights)


CCOLS = 512


def combine_kernel(c_ref, x_ref, mid_ref, o_ref):
    both = dot_nn(c_ref[...], x_ref[...])
    o_ref[...] = (mid_ref[...].astype(F32) + (both[:TOK] + both[TOK:])).astype(BF16)


def combine(matrix, rows, middle):
    return pl.pallas_call(
        combine_kernel,
        grid=(D // CCOLS,),
        out_shape=jax.ShapeDtypeStruct((TOK, D), BF16),
        in_specs=[
            pl.BlockSpec((2 * TOK, SLOTS), lambda i: (0, 0)),
            pl.BlockSpec((SLOTS, CCOLS), lambda i: (0, i)),
            pl.BlockSpec((TOK, CCOLS), lambda i: (0, i)),
        ],
        out_specs=pl.BlockSpec((TOK, CCOLS), lambda i: (0, i)),
        compiler_params=pltpu.CompilerParams(vmem_limit_bytes=48 * MIB),
        name="combine",
    )(matrix, rows, middle)


DROWS = KVH * 8


def pieces_of(x, count):
    pieces = []
    for _ in range(count):
        piece = x.astype(BF16).astype(F32)
        pieces.append(piece)
        x = x - piece
    return pieces


def decode_kernel(info_ref, q_ref, kn_ref, vn_ref, k_ref, v_ref, o_ref):
    request = pl.program_id(0)
    seq = info_ref[0]
    length = info_ref[1 + request]
    query = q_ref[0]
    position = seq * CBLK + lax.broadcasted_iota(jnp.int32, (DROWS, CBLK), 1)
    visible = position < length
    scores = jnp.where(visible, dot_nt(query, k_ref[0]) * SCALE, NEGATIVE)
    first = jnp.where(seq == 0, 1.0, 0.0)
    product = query.astype(F32) * kn_ref[0].astype(F32)
    fresh = jnp.sum(product, axis=1, keepdims=True) * SCALE
    fresh = jnp.where(first > 0.5, fresh, NEGATIVE)
    top = jnp.maximum(jnp.max(scores, axis=1, keepdims=True), fresh)
    weights = jnp.where(visible, jnp.exp(scores - top), 0.0)
    fresh_weight = jnp.exp(fresh - top) * first
    total = jnp.sum(weights, axis=1, keepdims=True) + fresh_weight
    fresh_round = fresh_weight.astype(BF16).astype(F32)
    weighted = dot_nn(weights.astype(BF16), v_ref[0]) + fresh_round * vn_ref[0].astype(F32)
    weighted = weighted / jnp.maximum(total, 1e-30)
    stats = pieces_of(top, 3) + pieces_of(total, 3)
    lane = lax.broadcasted_iota(jnp.int32, (DROWS, 128), 1)
    packed = jnp.zeros((DROWS, 128), F32)
    for number, piece in enumerate(stats):
        packed = jnp.where(lane >= HD + 8 * number, piece, packed)
    lane = lax.broadcasted_iota(jnp.int32, (8, 128), 1)
    for kv in range(KVH):
        rows = slice(8 * kv, 8 * kv + 8)
        lanes = slice(128 * (kv // 2), 128 * (kv // 2) + 128)
        piece = weighted[rows, lanes]
        if kv % 2:
            piece = swap_halves(piece)
        o_ref[kv] = jnp.where(lane < HD, piece, packed[rows]).astype(BF16)


def decode(info, query, key_new, value_new, key_cache, value_cache):
    return pl.pallas_call(
        decode_kernel,
        grid=(RLOC,),
        out_shape=jax.ShapeDtypeStruct((SEQ, 8, 128), BF16),
        in_specs=[
            pl.BlockSpec(memory_space=pltpu.SMEM),
            pl.BlockSpec((1, DROWS, KVH * HD), lambda i: (i, 0, 0)),
            pl.BlockSpec((1, 1, KVH * HD), lambda i: (i, 0, 0)),
            pl.BlockSpec((1, 1, KVH * HD), lambda i: (i, 0, 0)),
            pl.BlockSpec((1, CBLK, KVH * HD), lambda i: (i, 0, 0)),
            pl.BlockSpec((1, CBLK, KVH * HD), lambda i: (i, 0, 0)),
        ],
        out_specs=pl.BlockSpec((KVH, 8, 128), lambda i: (i, 0, 0)),
        compiler_params=pltpu.CompilerParams(vmem_limit_bytes=48 * MIB),
        name="decode",
    )(info, query, key_new, value_new, key_cache, value_cache)


def exchange(x):
    return lax.all_to_all(x, "seq", split_axis=0, concat_axis=0, tiled=True)


def gather_seq(tile):
    seq = lax.axis_index("seq")
    tiles = tile[None]
    for step in (1, 2, 4, 8, 16):
        other = lax.ppermute(tiles, "seq", [(i, i ^ step) for i in range(SEQ)])
        upper = (seq & step) != 0
        tiles = jnp.concatenate(
            [jnp.where(upper, other, tiles), jnp.where(upper, tiles, other)], axis=0
        )
    return tiles


def join_req(own, pair, far, far_pair):
    index = lax.axis_index("req")
    size = own.shape[0]
    full = jnp.zeros((4 * size, own.shape[1]), own.dtype)
    for piece, flip in ((own, 0), (pair, 1), (far, 2), (far_pair, 3)):
        full = lax.dynamic_update_slice_in_dim(full, piece, (index ^ flip) * size, 0)
    return full


def merge_decode(tails):
    values = tails.astype(F32)
    stats = values[:, :, HD : HD + 48].reshape(SEQ, 8, 6, 8)[..., 0]
    tops = jnp.sum(stats[..., :3], axis=-1, keepdims=True)
    totals = jnp.sum(stats[..., 3:], axis=-1, keepdims=True)
    weights = totals * jnp.exp(tops - jnp.max(tops, axis=0, keepdims=True))
    merged = jnp.sum(values[:, :, :HD] * weights, axis=0) / jnp.sum(weights, axis=0)
    return jnp.pad(merged.astype(BF16), ((0, 0), (0, 128 - HD)))


def block_query(dec_query):
    rows = dec_query.reshape(RLOC, KVH, GROUP, HD)
    rows = jnp.pad(rows, ((0, 0), (0, 0), (0, 8 - GROUP), (0, 0)))
    same = jnp.eye(KVH, dtype=BF16)[None, :, None, :, None]
    return (rows[:, :, :, None, :] * same).reshape(RLOC, DROWS, KVH * HD)


def body(
    prefill_query,
    prefill_key,
    prefill_value,
    prefill_resid,
    dec_query,
    dec_key_new,
    dec_value_new,
    dec_resid,
    cache_lengths,
    key_cache,
    value_cache,
    attn_out_weight,
    ffn_gain,
    expert_gate,
    expert_up,
    expert_down,
    routes,
    route_weights,
):
    seq = lax.axis_index("seq").astype(jnp.int32)
    strip = (seq % PARTS).reshape(1)
    own = jnp.concatenate([expert_gate[0], expert_up[0], expert_down[0].T], axis=1)
    near = [(i, i ^ 1) for i in range(4)]
    far = lax.ppermute(own, "req", [(i, i ^ 2) for i in range(4)])
    received = exchange(pack(prefill_query, prefill_key, prefill_value))
    spread, matrix = route(routes, route_weights)
    info = jnp.concatenate([seq.reshape(1), cache_lengths])
    partial = decode(
        info,
        block_query(dec_query),
        dec_key_new.reshape(RLOC, 1, KVH * HD),
        dec_value_new.reshape(RLOC, 1, KVH * HD),
        key_cache,
        value_cache,
    )
    received, partial, spread, matrix = lax.optimization_barrier(
        (received, partial, spread, matrix)
    )
    attended = exchange(attention(strip, received, partial))
    attended, far = lax.optimization_barrier((attended, far))
    middle, outgoing = post(attended, attn_out_weight, prefill_resid, ffn_gain[None, :], spread)
    outgoing, far, own, tails = lax.optimization_barrier(
        (outgoing, far, own, attended[:, QROWS:, :])
    )
    incoming = exchange(outgoing.reshape(EXPERTS, CAP, D)).reshape(SLOTS, D)
    weights = join_req(own, lax.ppermute(own, "req", near), far, lax.ppermute(far, "req", near))
    decoded = gather_seq(merge_decode(tails))
    incoming, weights = lax.optimization_barrier((incoming, weights))
    result = expert(incoming, weights)
    returned = exchange(result.reshape(EXPERTS, CAP, D)).reshape(SLOTS, D)
    decoded = decoded[:, :GROUP, :HD].reshape(RLOC, HEADS * HD)
    dec_out = (
        dec_resid.astype(F32) + jnp.dot(decoded, attn_out_weight, preferred_element_type=F32)
    ).astype(BF16)
    prefill_out = combine(matrix, returned, middle)
    return (prefill_out, dec_out)


def solution(mesh):
    return jax.shard_map(
        body,
        mesh=mesh,
        in_specs=(
            P(("req", "seq"), None),
            P(("req", "seq"), None),
            P(("req", "seq"), None),
            P(("req", "seq"), None),
            P("req", None),
            P("req", None),
            P("req", None),
            P("req", None),
            P("req"),
            P("req", "seq", None),
            P("req", "seq", None),
            P(),
            P(),
            P("seq", "req", None),
            P("seq", "req", None),
            P("seq", None, "req"),
            P(("req", "seq"), None),
            P(("req", "seq"), None),
        ),
        out_specs=(P(("req", "seq"), None), P("req", None)),
        check_vma=False,
    )
```
